32 devices in a mesh: fsdp: 8 (over y, x, core), tp: 4 (over z).
Axes of the slice: x: 2, y: 2, z: 4, core: 2. Of those that a mesh axis runs over, the one named last changes fastest.
Arguments:
- tokens: bfloat16 [2, 8, 1024, 2048], P(None, 'fsdp', 'tp'), may hold values from -6 to 6
- segment: int32 [2, 8, 1024], P(None, 'fsdp'), may hold values from 0 to 7, never falling along the last dimension, each value on 1 to 512 neighbouring positions
- ln1_gain: float32 [2048], P(('fsdp', 'tp')), may hold values from 0.5 to 1.5
- ln1_bias: float32 [2048], P(('fsdp', 'tp')), may hold values from -1.5 to 1.5
- w_query: bfloat16 [2048, 2048], P('fsdp', 'tp'), may hold values from -0.125 to 0.125
- w_key: bfloat16 [2048, 2048], P('fsdp', 'tp'), may hold values from -0.125 to 0.125
- w_value: bfloat16 [2048, 4096], P('fsdp', 'tp'), may hold values from -0.125 to 0.125
- w_gate: bfloat16 [2048, 4096], P('fsdp', 'tp'), may hold values from -0.125 to 0.125
- w_output: bfloat16 [4096, 2048], P('tp', 'fsdp'), may hold values from -0.09375 to 0.09375
- gn_gain: float32 [4096], P(('fsdp', 'tp')), may hold values from 0.5 to 1.5
- gn_bias: float32 [4096], P(('fsdp', 'tp')), may hold values from -1.5 to 1.5
- ln2_gain: float32 [2048], P(('fsdp', 'tp')), may hold values from 0.5 to 1.5
- ln2_bias: float32 [2048], P(('fsdp', 'tp')), may hold values from -1.5 to 1.5
- w_inner: bfloat16 [2048, 4096], P('fsdp', 'tp'), may hold values from -0.125 to 0.125
- b_inner: float32 [4096], P(('fsdp', 'tp')), may hold values from -1.5 to 1.5
- w_outer: bfloat16 [4096, 2048], P('tp', 'fsdp'), may hold values from -0.09375 to 0.09375
- b_outer: float32 [2048], P(('fsdp', 'tp')), may hold values from -1.5 to 1.5
- cotangent: bfloat16 [2, 8, 1024, 2048], P(None, 'fsdp', 'tp'), may hold values from -6 to 6
Outputs:
- out: bfloat16 [2, 8, 1024, 2048], P(None, 'fsdp', 'tp')
- input_grad: float32 [2, 8, 1024, 2048], P(None, 'fsdp', 'tp')
- grad_ln1_gain: float32 [2048], P(('fsdp', 'tp'))
- grad_ln1_bias: float32 [2048], P(('fsdp', 'tp'))
- grad_w_query: float32 [2048, 2048], P('fsdp', 'tp')
- grad_w_key: float32 [2048, 2048], P('fsdp', 'tp')
- grad_w_value: float32 [2048, 4096], P('fsdp', 'tp')
- grad_w_gate: float32 [2048, 4096], P('fsdp', 'tp')
- grad_w_output: float32 [4096, 2048], P('tp', 'fsdp')
- grad_gn_gain: float32 [4096], P(('fsdp', 'tp'))
- grad_gn_bias: float32 [4096], P(('fsdp', 'tp'))
- grad_ln2_gain: float32 [2048], P(('fsdp', 'tp'))
- grad_ln2_bias: float32 [2048], P(('fsdp', 'tp'))
- grad_w_inner: float32 [2048, 4096], P('fsdp', 'tp')
- grad_b_inner: float32 [4096], P(('fsdp', 'tp'))
- grad_w_outer: float32 [4096, 2048], P('tp', 'fsdp')
- grad_b_outer: float32 [2048], P(('fsdp', 'tp'))
The draws below stay inside these ranges and needn't reach their ends.
Inputs may be any that keep to these rules, and one draw needn't show every extreme that they name: `segment`: along a sequence the document numbers never fall; a document spans 1 to 512 tokens.
All inputs are finite; a program needn't handle non-finite values.
Results may differ from the reference program's by a relative error of at most 0.018.
Values may be sent and summed in bfloat16 or wider, within the bound.
A program may use at most 320 MiB of HBM per device.

```python
import math
import jax
import jax.numpy as jnp
import numpy as np
from jax import lax

D = 2048
HEADS = 8
DK = 256
DV = 512
FF = 4096
LEN = 1024
STRETCH = 512
MB = 2
SEQS = 8


def shard_levels(key, dims, split, least, largest):
    def one(dim, shards_of):
        heights = jax.random.uniform(jax.random.fold_in(jax.random.fold_in(key, 6), dim), (shards_of,), jnp.float32, least / len(split), largest / len(split))
        return jnp.repeat(jnp.exp(heights), dims[dim] // shards_of).reshape((-1,) + (1,) * (len(dims) - dim - 1))

    factor_of = one(*split[0])
    for cut in split[1:]:
        factor_of = factor_of * one(*cut)
    return factor_of


def profile(amount, total, most, slope):
    loads = [(1 << 20) // math.isqrt(standing ** slope) + 1 for standing in range(2, amount + 1)]
    spare, given = total - most - (amount - 1), [1] * (amount - 1)
    while spare > 0:
        candidates = [i for i in range(amount - 1) if given[i] < most]
        whole, budget = sum([loads[i] for i in candidates]), spare
        for i in candidates:
            more = min(most - given[i], max(1, budget * loads[i] // whole), spare)
            given[i] = given[i] + more
            spare = spare - more
    return np.array([most] + given)


def uneven_parts(own_key, count, total, most, lean):
    if count == 2:
        one = jax.random.randint(own_key, (), max(1, total - most), min(most, total - 1) + 1)
        return jnp.stack([one, total - one])
    lengths = jnp.asarray(profile(count, total, most, lean), jnp.int32)
    pairs = (count - 1) // 2
    source_of, sink = lengths[1:1 + 2 * pairs:2], lengths[2:2 + 2 * pairs:2]
    slack = jnp.minimum(source_of - 1, most - sink)
    shifted = jax.random.randint(jax.random.fold_in(own_key, 1), (pairs,), 0, 1 << 20) % (slack + 1)
    lengths = lengths.at[1:1 + 2 * pairs:2].set(source_of - shifted).at[2:2 + 2 * pairs:2].set(sink + shifted)
    return lengths[jax.random.permutation(jax.random.fold_in(own_key, 2), count)]


def bell_draw(key, shape, scale, most, split=(), kind=jnp.bfloat16):
    factor_of = shard_levels(key, shape, split, -0.22, 0.18) if split else 1.0
    entries = jax.random.normal(key, shape, jnp.float32) * scale * factor_of
    return jnp.minimum(jnp.maximum(entries, -most), most).astype(kind)


def setup_inputs(seed: int = 0) -> dict:
    seeds = jax.random.split(jax.random.key(seed), 19)
    tokens = bell_draw(seeds[0], (MB, SEQS, LEN, D), 1.0, 6.0, ((1, 8), (2, 4)))
    segment = jax.vmap(lambda own: jnp.searchsorted(jnp.cumsum(uneven_parts(own, max(LEN // 128, 4), LEN, LEN // 2, 2)), jnp.arange(LEN), side="right"))(jax.random.split(seeds[1], MB * SEQS)).reshape((MB, SEQS, LEN)).astype(jnp.int32)
    ln1_gain = jnp.clip(1.0 + 0.1 * jax.random.normal(seeds[2], (D,), jnp.float32), 0.5, 1.5)
    ln1_bias = bell_draw(seeds[3], (D,), 0.3, 1.5, ((0, 32),), jnp.float32)
    w_query = bell_draw(seeds[4], (D, D), D ** -0.5, 0.125, ((0, 8), (1, 4)))
    w_key = bell_draw(seeds[5], (D, D), D ** -0.5, 0.125, ((0, 8), (1, 4)))
    w_value = bell_draw(seeds[6], (D, 2 * D), D ** -0.5, 0.125, ((0, 8), (1, 4)))
    w_gate = bell_draw(seeds[7], (D, 2 * D), D ** -0.5, 0.125, ((0, 8), (1, 4)))
    w_output = bell_draw(seeds[8], (2 * D, D), (2 * D) ** -0.5, 0.09375, ((0, 4), (1, 8)))
    gn_gain = jnp.clip(1.0 + 0.1 * jax.random.normal(seeds[9], (2 * D,), jnp.float32), 0.5, 1.5)
    gn_bias = bell_draw(seeds[10], (2 * D,), 0.3, 1.5, ((0, 32),), jnp.float32)
    ln2_gain = jnp.clip(1.0 + 0.1 * jax.random.normal(seeds[11], (D,), jnp.float32), 0.5, 1.5)
    ln2_bias = bell_draw(seeds[12], (D,), 0.3, 1.5, ((0, 32),), jnp.float32)
    w_inner = bell_draw(seeds[13], (D, FF), D ** -0.5, 0.125, ((0, 8), (1, 4)))
    b_inner = bell_draw(seeds[14], (FF,), 0.3, 1.5, ((0, 32),), jnp.float32)
    w_outer = bell_draw(seeds[15], (FF, D), FF ** -0.5, 0.09375, ((0, 4), (1, 8)))
    b_outer = bell_draw(seeds[16], (D,), 0.3, 1.5, ((0, 32),), jnp.float32)
    cotangent = bell_draw(seeds[17], (MB, SEQS, LEN, D), 1.0, 6.0, ((1, 8), (2, 4)))
    return dict(tokens=tokens, segment=segment, ln1_gain=ln1_gain, ln1_bias=ln1_bias, w_query=w_query, w_key=w_key, w_value=w_value, w_gate=w_gate, w_output=w_output, gn_gain=gn_gain, gn_bias=gn_bias, ln2_gain=ln2_gain, ln2_bias=ln2_bias, w_inner=w_inner, b_inner=b_inner, w_outer=w_outer, b_outer=b_outer, cotangent=cotangent)


EPSILON = 1e-05
GROUP_EPSILON = 0.25

@jax.custom_vjp
def low(v):
    return lax.optimization_barrier(v.astype(jnp.bfloat16)).astype(jnp.float32)

@jax.custom_vjp
def low_back(v):
    return v

def low_keep(v):
    return (low(v), None)

def low_pass(kept, grad):
    return (grad,)

def back_keep(v):
    return (v, None)

def back_low(kept, grad):
    return (low(grad),)
low.defvjp(low_keep, low_pass)
low_back.defvjp(back_keep, back_low)

def matmul_high(left, right):
    return jnp.dot(left, right, precision=lax.Precision.HIGHEST, preferred_element_type=jnp.float32)

def einsum_full_precision(formula, left, right):
    return jnp.einsum(formula, left, right, precision=lax.Precision.HIGHEST, preferred_element_type=jnp.float32)

def layer_norm(values, scaling, offset):
    centred = values - lax.optimization_barrier(jnp.mean(values, axis=-1, keepdims=True))
    variance = lax.optimization_barrier(jnp.mean(centred * centred, axis=-1, keepdims=True))
    return centred * lax.rsqrt(variance + EPSILON) * scaling + offset

def gate_norm(retained, gate_pre, scaling, offset):
    length = retained.shape[0]
    centred = retained - lax.optimization_barrier(jnp.mean(retained, axis=-1, keepdims=True))
    variance = lax.optimization_barrier(jnp.mean(centred * centred, axis=-1, keepdims=True))
    grouped = (centred * lax.rsqrt(variance + GROUP_EPSILON)).reshape(length, -1) * scaling + offset
    return gate_pre * jax.nn.sigmoid(gate_pre) * grouped

def rotate(values, position, turning):
    half_dim = values.shape[-1] // 2
    frequency = 10000.0 ** (-jnp.arange(half_dim, dtype=jnp.float32) / half_dim)
    angles = position[:, None] * frequency[None, :] * turning
    cosine = jnp.cos(angles)[:, None, :]
    sinusoid = jnp.sin(angles)[:, None, :]
    leading = values[..., :half_dim]
    trailing = values[..., half_dim:]
    return jnp.concatenate([leading * cosine - trailing * sinusoid, leading * sinusoid + trailing * cosine], axis=-1)

def doc_positions(segments):
    length = segments.shape[0]
    indices = jnp.arange(length, dtype=jnp.int32)
    previous = jnp.concatenate([jnp.full((1,), -1, jnp.int32), segments[:-1].astype(jnp.int32)])
    starts = lax.cummax(jnp.where(segments != previous, indices, 0), axis=0)
    return (indices - starts).astype(jnp.float32)

def decay_mask(first_row, segments, log_decay):
    row_ids = first_row + jnp.arange(STRETCH, dtype=jnp.int32)
    columns = jnp.arange(segments.shape[0], dtype=jnp.int32)
    seg_query = lax.dynamic_slice_in_dim(segments, first_row, STRETCH, 0)
    distance = row_ids[:, None] - columns[None, :]
    allowed = (distance >= 0) & (seg_query[:, None] == segments[None, :])
    steps_back = jnp.maximum(distance, 0).astype(jnp.float32)
    return jnp.where(allowed[None], jnp.exp(steps_back[None] * log_decay[:, None, None]), 0.0)

def retention(query_low, key_rounded, value_rounded, segments, log_decay):
    length = query_low.shape[0]
    score_scale = DK ** (-0.5)

    def block(block_id):
        first_row = (block_id * STRETCH).astype(jnp.int32)
        query_tile_rows = lax.dynamic_slice_in_dim(query_low, first_row, STRETCH, 0)
        masking = decay_mask(first_row, segments, log_decay)
        retention_scores = low_back(einsum_full_precision('awx,bwx->wab', query_tile_rows, key_rounded))
        weights_low = low(retention_scores * masking * score_scale)
        return einsum_full_precision('hnm,mhe->nhe', weights_low, value_rounded)
    blocks = lax.map(jax.checkpoint(block), jnp.arange(length // STRETCH, dtype=jnp.int32))
    return blocks.reshape(length, query_low.shape[1], value_rounded.shape[2])

def forward_seq(token_seq, segments, weights):
    norm1_gain, norm1_bias, query_w, key_w, value_w, gate_w, output_w, group_gain, group_bias, norm2_gain, second_norm_bias, inner_w, inner_bias, outer_w, outer_bias = weights
    position = doc_positions(segments)
    log_decay = jnp.log1p(-2.0 ** (-5.0 - jnp.arange(HEADS, dtype=jnp.float32)))
    normed_one = low(layer_norm(token_seq, norm1_gain, norm1_bias))
    query_low = low(rotate(low_back(matmul_high(normed_one, query_w)).reshape(LEN, HEADS, DK), position, 1.0))
    key_rounded = low(rotate(low_back(matmul_high(normed_one, key_w)).reshape(LEN, HEADS, DK), position, 1.0))
    value_rounded = low(low_back(matmul_high(normed_one, value_w))).reshape(LEN, HEADS, DV)
    retained = low_back(retention(query_low, key_rounded, value_rounded, segments, log_decay))
    gate_pre = low_back(matmul_high(normed_one, gate_w))
    gated = low(gate_norm(retained, gate_pre, group_gain, group_bias))
    hidden = token_seq + low_back(matmul_high(gated, output_w))
    normed_two = low(layer_norm(hidden, norm2_gain, second_norm_bias))
    inner = low_back(matmul_high(normed_two, inner_w) + inner_bias)
    active = low(jax.nn.gelu(inner, approximate=False))
    return hidden + low_back(matmul_high(active, outer_w)) + outer_bias

def reference(tokens, segment, ln1_gain, ln1_bias, w_query, w_key, w_value, w_gate, w_output, gn_gain, gn_bias, ln2_gain, ln2_bias, w_inner, b_inner, w_outer, b_outer, cotangent):
    params = tuple((item.astype(jnp.float32) for item in (ln1_gain, ln1_bias, w_query, w_key, w_value, w_gate, w_output, gn_gain, gn_bias, ln2_gain, ln2_bias, w_inner, b_inner, w_outer, b_outer)))
    count_seqs = MB * SEQS
    flat_tokens = tokens.reshape(count_seqs, LEN, D).astype(jnp.float32)
    flat_segments = segment.reshape(count_seqs, LEN).astype(jnp.int32)
    flat_cotangent = cotangent.reshape(count_seqs, LEN, D).astype(jnp.float32)

    def step(totals, item):
        token_seq, segment_seq, cotangent_seq = item

        def forward(values, weights):
            return forward_seq(values, segment_seq, weights)
        result, pullback = jax.vjp(forward, token_seq, params)
        input_part, param_grads = pullback(cotangent_seq)
        summed = tuple((total + grad_part for total, grad_part in zip(totals, param_grads)))
        return (summed, (result.astype(jnp.bfloat16), input_part))
    starting = tuple((jnp.zeros_like(item) for item in params))
    totals, (outputs, input_grads) = lax.scan(step, starting, (flat_tokens, flat_segments, flat_cotangent))
    return (outputs.reshape(tokens.shape), input_grads.reshape(tokens.shape), totals[0], totals[1], totals[2], totals[3], totals[4], totals[5], totals[6], totals[7], totals[8], totals[9], totals[10], totals[11], totals[12], totals[13], totals[14])
```

```python
import functools

import jax
import jax.numpy as jnp
from jax import lax
from jax.experimental import pallas as pl
from jax.experimental.pallas import tpu as pltpu
from jax.sharding import PartitionSpec as P

DK = 256
DV = 512
ROWS = 256

EPSILON = 1e-05
GROUP_EPSILON = 0.25
BF16 = jnp.bfloat16
F32 = jnp.float32


def layer_norm(values, scaling, offset):
    centred = values - jnp.mean(values, axis=-1, keepdims=True)
    variance = jnp.mean(centred * centred, axis=-1, keepdims=True)
    return centred * lax.rsqrt(variance + EPSILON) * scaling + offset


def doc_positions(segments):
    length = segments.shape[0]
    indices = jnp.arange(length, dtype=jnp.int32)
    previous = jnp.concatenate([jnp.full((1,), -1, jnp.int32), segments[:-1]])
    starts = lax.cummax(jnp.where(segments != previous, indices, 0), axis=0)
    return (indices - starts).astype(F32)


def dot_nn(left, right):
    return lax.dot_general(left, right, (((1,), (0,)), ((), ())), preferred_element_type=F32)


def dot_nt(left, right):
    return lax.dot_general(left, right, (((1,), (1,)), ((), ())), preferred_element_type=F32)


def dot_tn(left, right):
    return lax.dot_general(left, right, (((0,), (0,)), ((), ())), preferred_element_type=F32)


def turn(lead, trail, cosine, sinusoid):
    return jnp.concatenate(
        [lead * cosine - trail * sinusoid, lead * sinusoid + trail * cosine], axis=-1
    ).astype(BF16)


def mask_of(key_rows, key_cols, decay, length):
    gap = key_rows - key_cols
    inside = (gap >= 0.0) & (gap < length)
    return jnp.where(inside, jnp.exp(gap * decay), 0.0)


def retain_kernel(
    decay_ref, keyr_ref, keyc_ref, cos_ref, sin_ref, q_ref, k_ref, v_ref, g_ref, gain_ref, bias_ref, held_ref,
    gated_ref, kept_ref, qr_ref, kr_ref, vb_ref,
):
    del held_ref
    decay = decay_ref[pl.program_id(0)]
    length = q_ref.shape[0]
    half = DK // 2
    scale = DK ** (-0.5)
    qr_ref[...] = turn(q_ref[:, :half], q_ref[:, half:], cos_ref[...], sin_ref[...])
    kr_ref[...] = turn(k_ref[:, :half], k_ref[:, half:], cos_ref[...], sin_ref[...])
    vb_ref[...] = v_ref[...].astype(BF16)
    for first in range(0, length, ROWS):
        rows = pl.ds(first, ROWS)
        mask = mask_of(keyr_ref[rows, :], keyc_ref[...], decay, float(length))
        scores = dot_nt(qr_ref[rows, :], kr_ref[...])
        weights = (scores * mask * scale).astype(BF16)
        retained = dot_nn(weights, vb_ref[...])
        kept_ref[rows, :] = retained
        centred = retained - jnp.mean(retained, axis=-1, keepdims=True)
        variance = jnp.mean(centred * centred, axis=-1, keepdims=True)
        grouped = centred * lax.rsqrt(variance + GROUP_EPSILON) * gain_ref[...] + bias_ref[...]
        gate = g_ref[rows, :]
        gated_ref[rows, :] = (gate * jax.nn.sigmoid(gate) * grouped).astype(BF16)


def retain(decays, keyr, keyc, cosine, sinusoid, pre, gain, bias, held, place, heads):
    length = pre.shape[0]
    whole = lambda shape: pl.BlockSpec(shape, lambda h: (0,) * len(shape))
    cols = lambda width, start: pl.BlockSpec((length, width), lambda h: (0, start + h))
    vec = pl.BlockSpec((1, DV), lambda h: (0, h))
    return pl.pallas_call(
        retain_kernel,
        grid=(heads,),
        in_specs=[
            pl.BlockSpec(memory_space=pltpu.SMEM),
            whole((length, 1)), whole((1, length)),
            whole((length, DK // 2)), whole((length, DK // 2)),
            cols(DK, 0), cols(DK, heads), cols(DV, heads), cols(DV, 2 * heads),
            vec, vec,
            pl.BlockSpec(memory_space=pl.ANY),
        ],
        out_specs=[cols(DV, place * heads), cols(DV, 0), cols(DK, 0), cols(DK, 0), cols(DV, 0)],
        out_shape=[
            jax.ShapeDtypeStruct(held.shape, BF16),
            jax.ShapeDtypeStruct((length, heads * DV), F32),
            jax.ShapeDtypeStruct((length, heads * DK), BF16),
            jax.ShapeDtypeStruct((length, heads * DK), BF16),
            jax.ShapeDtypeStruct((length, heads * DV), BF16),
        ],
        input_output_aliases={11: 0},
        cost_estimate=pl.CostEstimate(
            flops=2 * heads * length * length * (DK + DV),
            bytes_accessed=heads * length * (2 * DK * 6 + DV * 16),
            transcendentals=heads * length * length,
        ),
        name="retain",
    )(decays, keyr, keyc, cosine, sinusoid, pre, pre, pre, pre, gain, bias, held)


def retain_back_kernel(
    decay_ref, keyr_ref, keyc_ref, cos_ref, sin_ref, qr_ref, kr_ref, vb_ref, g_ref, kept_ref, up_ref, gain_ref, bias_ref,
    grad_ref, dgain_ref, dbias_ref,
    dv_acc, dk_acc,
):
    head = pl.program_id(0)
    heads = pl.num_programs(0)
    decay = decay_ref[head]
    length = qr_ref.shape[0]
    half = DK // 2
    scale = DK ** (-0.5)
    at_q = pl.multiple_of(head * DK, DK)
    at_k = pl.multiple_of((heads + head) * DK, DK)
    at_v = pl.multiple_of((heads + head) * DV, DV)
    at_g = pl.multiple_of((2 * heads + head) * DV, DV)
    gain = gain_ref[...]
    bias = bias_ref[...]
    dgain = jnp.zeros((1, DV), F32)
    dbias = jnp.zeros((1, DV), F32)
    for first in range(0, length, ROWS):
        rows = pl.ds(first, ROWS)
        retained = kept_ref[rows, :]
        centred = retained - jnp.mean(retained, axis=-1, keepdims=True)
        variance = jnp.mean(centred * centred, axis=-1, keepdims=True)
        inverse = lax.rsqrt(variance + GROUP_EPSILON)
        unit = centred * inverse
        gate = g_ref[rows, :]
        open_gate = jax.nn.sigmoid(gate)
        up = up_ref[rows, :]
        grouped_grad = up * (gate * open_gate)
        gate_grad = up * (unit * gain + bias) * (open_gate * (1.0 + gate * (1.0 - open_gate)))
        grad_ref[rows, pl.ds(at_g, DV)] = gate_grad.astype(BF16)
        dgain = dgain + jnp.sum(grouped_grad * unit, axis=0, keepdims=True)
        dbias = dbias + jnp.sum(grouped_grad, axis=0, keepdims=True)
        unit_grad = grouped_grad * gain
        along = jnp.mean(unit_grad * unit, axis=-1, keepdims=True)
        level = jnp.mean(unit_grad, axis=-1, keepdims=True)
        retained_grad = (inverse * (unit_grad - level - unit * along)).astype(BF16)
        mask = mask_of(keyr_ref[rows, :], keyc_ref[...], decay, float(length)) * scale
        query = qr_ref[rows, :]
        weights = (dot_nt(query, kr_ref[...]) * mask).astype(BF16)
        value_part = dot_tn(weights, retained_grad)
        score_grad = (dot_nt(retained_grad, vb_ref[...]) * mask).astype(BF16)
        query_grad = dot_nn(score_grad, kr_ref[...])
        key_part = dot_tn(score_grad, query)
        if first == 0:
            dv_acc[...] = value_part
            dk_acc[...] = key_part
        else:
            dv_acc[...] += value_part
            dk_acc[...] += key_part
        grad_ref[rows, pl.ds(at_q, DK)] = turn(
            query_grad[:, :half], query_grad[:, half:], cos_ref[rows, :], -sin_ref[rows, :]
        )
    grad_ref[:, pl.ds(at_k, DK)] = turn(dk_acc[:, :half], dk_acc[:, half:], cos_ref[...], -sin_ref[...])
    grad_ref[:, pl.ds(at_v, DV)] = dv_acc[...].astype(BF16)
    dgain_ref[...] = dgain
    dbias_ref[...] = dbias


def retain_back(decays, keyr, keyc, cosine, sinusoid, qr, kr, vb, pre, kept, up, gain, bias, place, heads):
    length = pre.shape[0]
    whole = lambda shape: pl.BlockSpec(shape, lambda h: (0,) * len(shape))
    cols = lambda width, start: pl.BlockSpec((length, width), lambda h: (0, start + h))
    vec = pl.BlockSpec((1, DV), lambda h: (0, h))
    return pl.pallas_call(
        retain_back_kernel,
        grid=(heads,),
        in_specs=[
            pl.BlockSpec(memory_space=pltpu.SMEM),
            whole((length, 1)), whole((1, length)),
            whole((length, DK // 2)), whole((length, DK // 2)),
            cols(DK, 0), cols(DK, 0), cols(DV, 0), cols(DV, 2 * heads), cols(DV, 0), cols(DV, place * heads),
            vec, vec,
        ],
        out_specs=[whole((length, heads * 2 * (DK + DV))), vec, vec],
        out_shape=[
            jax.ShapeDtypeStruct((length, heads * 2 * (DK + DV)), BF16),
            jax.ShapeDtypeStruct((1, heads * DV), F32),
            jax.ShapeDtypeStruct((1, heads * DV), F32),
        ],
        scratch_shapes=[pltpu.VMEM((length, DV), F32), pltpu.VMEM((length, DK), F32)],
        cost_estimate=pl.CostEstimate(
            flops=2 * heads * length * length * (3 * DK + 2 * DV),
            bytes_accessed=heads * length * (2 * DK * 4 + DV * 18),
            transcendentals=heads * length * length,
        ),
        name="retain_back",
    )(decays, keyr, keyc, cosine, sinusoid, qr, kr, vb, pre, kept, up, gain, bias)


def shards(
    span, batches,
    tokens, segment, ln1_gain, ln1_bias, w_query, w_key, w_value, w_gate, w_output, gn_gain, gn_bias,
    ln2_gain, ln2_bias, w_inner, b_inner, w_outer, b_outer, cotangent,
):
    fsdp, tp = span
    teams = tp // batches
    devices = fsdp * tp
    place = lax.axis_index("tp")
    mine = place // teams
    rank = place % teams
    width = tokens.shape[3]
    piece = tokens.shape[2]
    heads = w_query.shape[1] // DK
    units = w_inner.shape[1]
    channels = w_value.shape[1]

    def along_team(value, shift):
        route = [
            (i, (i // teams) * teams + (i % teams + shift) % teams) for i in range(tp)
        ]
        return lax.ppermute(value, "tp", route)

    def across(value, shift):
        route = [
            (i, ((i // teams + shift) % batches) * teams + i % teams) for i in range(tp)
        ]
        return lax.ppermute(value, "tp", route)

    def quarter(back_batch, back_rank):
        return ((mine + batches - back_batch) % batches) * teams + (rank + teams - back_rank) % teams

    def pick(array, shift):
        return lax.dynamic_index_in_dim(array, (mine + shift) % batches, 0, keepdims=False)

    def own_rows(array):
        return jnp.concatenate(
            [pick(array, 0)[0]] + [across(pick(array, s)[0], s) for s in range(1, batches)], axis=0
        )

    def gather_team(value):
        return [value] + [along_team(value, s) for s in range(1, teams)]

    def scatter_team(part_of):
        sent = [along_team(part_of(s).astype(BF16), teams - s) for s in range(1, teams)]
        total = part_of(0)
        for received in sent:
            total = total + received.astype(F32)
        return total

    def give_back(rows):
        blocks = [rows[s * piece : (s + 1) * piece] for s in range(batches)]
        parts = [blocks[0]] + [
            across(blocks[s].astype(BF16), batches - s).astype(blocks[0].dtype) for s in range(1, batches)
        ]
        slots = []
        for i in range(batches):
            value = parts[0]
            for s in range(1, batches):
                value = jnp.where((mine + s) % batches == i, parts[s], value)
            slots.append(value)
        return jnp.stack(slots)[:, None]

    pieces = (ln1_gain, ln1_bias, ln2_gain, ln2_bias, b_outer, b_inner, gn_gain, gn_bias)
    flat = jnp.concatenate(pieces)
    used = flat.shape[0]
    lines = -(-used // 128)

    def exchange(table):
        padded = jnp.pad(table, ((0, 0), (0, lines * 128 - used))).reshape(devices, lines, 128)
        return lax.all_to_all(padded, ("fsdp", "tp"), 0, 0, tiled=True).reshape(devices, lines * 128)

    everyone = exchange(jnp.broadcast_to(flat[None], (devices, used)))
    vectors, begin = [], 0
    for item in pieces:
        vectors.append(everyone[:, begin : begin + item.shape[0]].reshape(-1))
        begin += item.shape[0]
    norm1_gain, norm1_bias, norm2_gain, norm2_bias, outer_bias, inner_all, group_gain_all, group_bias_all = vectors

    own_quarters = [quarter(s, 0) for s in range(batches)]

    def cut(vector, size):
        return [lax.dynamic_slice_in_dim(vector, q * size, size, 0) for q in own_quarters]

    inner_bias = jnp.concatenate(cut(inner_all, units))
    group_gains = [v[None] for v in cut(group_gain_all, channels)]
    group_biases = [v[None] for v in cut(group_bias_all, channels)]

    mixer_shard = jnp.concatenate([w_query, w_key, w_value, w_gate], axis=1)
    output_shard = w_output.T
    inner_shard = w_inner
    outer_shard = w_outer.T
    token_rows = own_rows(tokens)
    mixer_shards = [mixer_shard] + [across(mixer_shard, s) for s in range(1, batches)]
    mixers = [lax.all_gather(s, "fsdp", axis=0, tiled=True) for s in mixer_shards]

    def both(shard):
        return jnp.concatenate([shard] + [across(shard, s) for s in range(1, batches)], axis=1)

    output_full = lax.all_gather(both(output_shard), "fsdp", axis=0, tiled=True)
    inner_full = lax.all_gather(both(inner_shard), "fsdp", axis=0, tiled=True)
    outer_full = lax.all_gather(both(outer_shard), "fsdp", axis=0, tiled=True)
    grad_rows = own_rows(cotangent)
    grad_blocks = gather_team(grad_rows)

    segments = pick(segment, 0)[0]
    length = segments.shape[0]
    position = doc_positions(segments)
    order = [quarter(s, r) for r in range(teams) for s in range(batches)]

    def ordered(vector):
        return jnp.concatenate([lax.dynamic_slice_in_dim(vector, q * piece, piece, 0) for q in order])

    index = jnp.arange(length, dtype=jnp.int32)
    keys = ordered((segments * (2 * length) + index).astype(F32))
    keyr, keyc = keys[:, None], keys[None, :]
    frequency = 10000.0 ** (-jnp.arange(DK // 2, dtype=F32) / (DK // 2))
    angles = ordered(position)[:, None] * frequency[None, :]
    cosine, sinusoid = jnp.cos(angles), jnp.sin(angles)
    decays = [
        jnp.log1p(-(2.0 ** (-5.0 - (q * heads + jnp.arange(heads, dtype=jnp.int32)).astype(F32))))
        for q in own_quarters
    ]

    rows_in = token_rows.astype(F32)
    normed_one, norm1_back = jax.vjp(layer_norm, rows_in, norm1_gain, norm1_bias)
    normed_one_all = jnp.concatenate(gather_team(normed_one.astype(BF16)), axis=0)
    gated = jnp.zeros((length, batches * channels), BF16)
    saved = []
    for s in range(batches):
        pre = dot_nn(normed_one_all, mixers[s])
        gated, kept, qr, kr, vb = retain(
            decays[s], keyr, keyc, cosine, sinusoid, pre, group_gains[s], group_biases[s], gated, s, heads
        )
        saved.append((pre, kept, qr, kr, vb))
    block = batches * piece

    def rows_of(array, r):
        return array[r * block : (r + 1) * block]

    hidden = rows_in + scatter_team(lambda r: dot_nt(rows_of(gated, r), output_full))
    normed_two, norm2_back = jax.vjp(layer_norm, hidden, norm2_gain, norm2_bias)
    normed_two_blocks = gather_team(normed_two.astype(BF16))
    active_blocks, slope_blocks = [], []
    for normed in normed_two_blocks:
        inner = dot_nn(normed, inner_full) + inner_bias
        below = 0.5 * (1.0 + lax.erf(inner * (0.5**0.5)))
        active_blocks.append((inner * below).astype(BF16))
        bell = jnp.exp(-0.5 * inner * inner) * ((2.0 * jnp.pi) ** -0.5)
        slope_blocks.append((below + inner * bell).astype(BF16))

    inner_grad_blocks = [
        (slope.astype(F32) * dot_nn(grad, outer_full)).astype(BF16)
        for slope, grad in zip(slope_blocks, grad_blocks)
    ]
    normed_two_grad = scatter_team(lambda r: dot_nt(inner_grad_blocks[r], inner_full))
    hidden_part, norm2_gain_sum, norm2_bias_sum = norm2_back(normed_two_grad)
    hidden_grad = grad_rows.astype(F32) + hidden_part
    hidden_low_all = jnp.concatenate(gather_team(hidden_grad.astype(BF16)), axis=0)

    result = hidden + scatter_team(lambda r: dot_nt(active_blocks[r], outer_full)) + outer_bias
    out = give_back(result.astype(BF16))

    def reduce_columns(whole):
        return lax.psum_scatter(whole.astype(BF16), "fsdp", scatter_dimension=0, tiled=True)

    def settle(parts):
        total = parts[0].astype(F32)
        for s in range(1, batches):
            total = total + across(parts[s], batches - s).astype(F32)
        return total

    def settle_both(whole):
        size = whole.shape[1] // batches
        return settle([whole[:, s * size : (s + 1) * size] for s in range(batches)])

    active_all = jnp.concatenate(active_blocks, axis=0)
    grad_all = jnp.concatenate(grad_blocks, axis=0)
    inner_grad_all = jnp.concatenate(inner_grad_blocks, axis=0)
    normed_two_all = jnp.concatenate(normed_two_blocks, axis=0)
    grad_outer = settle_both(reduce_columns(dot_tn(grad_all, active_all))).T
    grad_inner = settle_both(reduce_columns(dot_tn(normed_two_all, inner_grad_all)))
    inner_bias_sum = jnp.sum(inner_grad_all.astype(F32), axis=0)
    outer_bias_sum = jnp.sum(grad_rows.astype(F32), axis=0)

    gated_grad = dot_nn(hidden_low_all, output_full)
    grads, gain_sums, bias_sums, mixer_sums = [], [], [], []
    for s in reversed(range(batches)):
        pre, kept, qr, kr, vb = saved[s]
        grad, gain_sum, bias_sum = retain_back(
            decays[s], keyr, keyc, cosine, sinusoid, qr, kr, vb, pre, kept, gated_grad,
            group_gains[s], group_biases[s], s, heads,
        )
        grads.insert(0, grad)
        gain_sums.insert(0, gain_sum[0])
        bias_sums.insert(0, bias_sum[0])
        mixer_sums.insert(0, reduce_columns(dot_tn(normed_one_all, grad)))
    grad_output = settle_both(reduce_columns(dot_tn(hidden_low_all, gated))).T

    def normed_one_part(r):
        total = dot_nt(rows_of(grads[0], r), mixers[0])
        for s in range(1, batches):
            total = total + dot_nt(rows_of(grads[s], r), mixers[s])
        return total

    normed_one_grad = scatter_team(normed_one_part)
    input_part, norm1_gain_sum, norm1_bias_sum = norm1_back(normed_one_grad)
    input_grad = give_back(hidden_grad + input_part)
    grad_mixer = settle(mixer_sums)
    narrow, wide = w_query.shape[1], channels
    grad_query = grad_mixer[:, :narrow]
    grad_key = grad_mixer[:, narrow : 2 * narrow]
    grad_value = grad_mixer[:, 2 * narrow : 2 * narrow + wide]
    grad_gate = grad_mixer[:, 2 * narrow + wide :]

    def spread(parts, size):
        total = jnp.zeros((tp * size,), F32)
        for q, part in zip(own_quarters, parts):
            total = lax.dynamic_update_slice_in_dim(total, part, q * size, 0)
        return total

    sums = (
        norm1_gain_sum,
        norm1_bias_sum,
        norm2_gain_sum,
        norm2_bias_sum,
        outer_bias_sum,
        spread([inner_bias_sum[s * units : (s + 1) * units] for s in range(batches)], units),
        spread(gain_sums, channels),
        spread(bias_sums, channels),
    )
    shared = jnp.sum(exchange(jnp.concatenate([v.reshape(devices, -1) for v in sums], axis=1)), axis=0)
    small, begin = [], 0
    for item in pieces:
        small.append(shared[begin : begin + item.shape[0]])
        begin += item.shape[0]
    return (
        out, input_grad, small[0], small[1], grad_query, grad_key, grad_value, grad_gate, grad_output,
        small[6], small[7], small[2], small[3], grad_inner, small[5], grad_outer, small[4],
    )


def solution(mesh):
    rows, vec = P(None, "fsdp", "tp", None), P(("fsdp", "tp"))
    tall, flat = P("fsdp", "tp"), P("tp", "fsdp")
    span = (mesh.shape["fsdp"], mesh.shape["tp"])

    def step(*args):
        return jax.shard_map(
            functools.partial(shards, span, args[0].shape[0]),
            mesh=mesh,
            in_specs=(
                rows, P(None, "fsdp", None), vec, vec, tall, tall, tall, tall, flat,
                vec, vec, vec, vec, tall, vec, flat, vec, rows,
            ),
            out_specs=(
                rows, rows, vec, vec, tall, tall, tall, tall, flat,
                vec, vec, vec, vec, tall, vec, flat, vec,
            ),
            check_vma=False,
        )(*args)

    return step
```

```python
import functools

import jax
import jax.numpy as jnp
from jax import lax
from jax.experimental import pallas as pl
from jax.experimental.pallas import tpu as pltpu
from jax.sharding import PartitionSpec as P

DK = 256
DV = 512
ROWS = 256

EPSILON = 1e-05
GROUP_EPSILON = 0.25
BF16 = jnp.bfloat16
F32 = jnp.float32


def layer_norm(values, scaling, offset):
    centred = values - jnp.mean(values, axis=-1, keepdims=True)
    variance = jnp.mean(centred * centred, axis=-1, keepdims=True)
    return centred * lax.rsqrt(variance + EPSILON) * scaling + offset


def doc_positions(segments):
    length = segments.shape[0]
    indices = jnp.arange(length, dtype=jnp.int32)
    previous = jnp.concatenate([jnp.full((1,), -1, jnp.int32), segments[:-1]])
    starts = lax.cummax(jnp.where(segments != previous, indices, 0), axis=0)
    return (indices - starts).astype(F32)


def dot_nn(left, right):
    return lax.dot_general(left, right, (((1,), (0,)), ((), ())), preferred_element_type=F32)


def dot_nt(left, right):
    return lax.dot_general(left, right, (((1,), (1,)), ((), ())), preferred_element_type=F32)


def dot_tn(left, right):
    return lax.dot_general(left, right, (((0,), (0,)), ((), ())), preferred_element_type=F32)


def hold(value, *others):
    return lax.optimization_barrier((value,) + others)[0]


def turn(lead, trail, cosine, sinusoid):
    return jnp.concatenate(
        [lead * cosine - trail * sinusoid, lead * sinusoid + trail * cosine], axis=-1
    ).astype(BF16)


def mask_of(key_rows, key_cols, decay, length):
    gap = key_rows - key_cols
    inside = (gap >= 0.0) & (gap < length)
    return jnp.where(inside, jnp.exp(gap * decay), 0.0)


def retain_kernel(
    decay_ref, keyr_ref, keyc_ref, cos_ref, sin_ref, q_ref, k_ref, v_ref, g_ref, gain_ref, bias_ref, held_ref,
    gated_ref, kept_ref, qr_ref, kr_ref, vb_ref,
):
    del held_ref
    decay = decay_ref[pl.program_id(0)]
    length = q_ref.shape[0]
    half = DK // 2
    scale = DK ** (-0.5)
    qr_ref[...] = turn(q_ref[:, :half], q_ref[:, half:], cos_ref[...], sin_ref[...])
    kr_ref[...] = turn(k_ref[:, :half], k_ref[:, half:], cos_ref[...], sin_ref[...])
    vb_ref[...] = v_ref[...].astype(BF16)
    for first in range(0, length, ROWS):
        rows = pl.ds(first, ROWS)
        mask = mask_of(keyr_ref[rows, :], keyc_ref[...], decay, float(length))
        scores = dot_nt(qr_ref[rows, :], kr_ref[...])
        weights = (scores * mask * scale).astype(BF16)
        retained = dot_nn(weights, vb_ref[...])
        kept_ref[rows, :] = retained
        centred = retained - jnp.mean(retained, axis=-1, keepdims=True)
        variance = jnp.mean(centred * centred, axis=-1, keepdims=True)
        grouped = centred * lax.rsqrt(variance + GROUP_EPSILON) * gain_ref[...] + bias_ref[...]
        gate = g_ref[rows, :]
        gated_ref[rows, :] = (gate * jax.nn.sigmoid(gate) * grouped).astype(BF16)


def retain(decays, keyr, keyc, cosine, sinusoid, pre, gain, bias, held, place, heads):
    length = pre.shape[0]
    whole = lambda shape: pl.BlockSpec(shape, lambda h: (0,) * len(shape))
    cols = lambda width, start: pl.BlockSpec((length, width), lambda h: (0, start + h))
    vec = pl.BlockSpec((1, DV), lambda h: (0, h))
    return pl.pallas_call(
        retain_kernel,
        grid=(heads,),
        in_specs=[
            pl.BlockSpec(memory_space=pltpu.SMEM),
            whole((length, 1)), whole((1, length)),
            whole((length, DK // 2)), whole((length, DK // 2)),
            cols(DK, 0), cols(DK, heads), cols(DV, heads), cols(DV, 2 * heads),
            vec, vec,
            pl.BlockSpec(memory_space=pl.ANY),
        ],
        out_specs=[cols(DV, place * heads), cols(DV, 0), cols(DK, 0), cols(DK, 0), cols(DV, 0)],
        out_shape=[
            jax.ShapeDtypeStruct(held.shape, BF16),
            jax.ShapeDtypeStruct((length, heads * DV), F32),
            jax.ShapeDtypeStruct((length, heads * DK), BF16),
            jax.ShapeDtypeStruct((length, heads * DK), BF16),
            jax.ShapeDtypeStruct((length, heads * DV), BF16),
        ],
        input_output_aliases={11: 0},
        cost_estimate=pl.CostEstimate(
            flops=2 * heads * length * length * (DK + DV),
            bytes_accessed=heads * length * (2 * DK * 6 + DV * 16),
            transcendentals=heads * length * length,
        ),
        name="retain",
    )(decays, keyr, keyc, cosine, sinusoid, pre, pre, pre, pre, gain, bias, held)


def retain_back_kernel(
    decay_ref, keyr_ref, keyc_ref, cos_ref, sin_ref, qr_ref, kr_ref, vb_ref, g_ref, kept_ref, gain_ref, bias_ref,
    *rest,
):
    *up_refs, grad_ref, dgain_ref, dbias_ref, dv_acc, dk_acc = rest
    block = up_refs[0].shape[0]
    head = pl.program_id(0)
    heads = pl.num_programs(0)
    decay = decay_ref[head]
    length = qr_ref.shape[0]
    half = DK // 2
    scale = DK ** (-0.5)
    at_q = pl.multiple_of(head * DK, DK)
    at_k = pl.multiple_of((heads + head) * DK, DK)
    at_v = pl.multiple_of((heads + head) * DV, DV)
    at_g = pl.multiple_of((2 * heads + head) * DV, DV)
    gain = gain_ref[...]
    bias = bias_ref[...]
    dgain = jnp.zeros((1, DV), F32)
    dbias = jnp.zeros((1, DV), F32)
    for first in range(0, length, ROWS):
        rows = pl.ds(first, ROWS)
        retained = kept_ref[rows, :]
        centred = retained - jnp.mean(retained, axis=-1, keepdims=True)
        variance = jnp.mean(centred * centred, axis=-1, keepdims=True)
        inverse = lax.rsqrt(variance + GROUP_EPSILON)
        unit = centred * inverse
        gate = g_ref[rows, :]
        open_gate = jax.nn.sigmoid(gate)
        up = up_refs[first // block][first % block : first % block + ROWS, :]
        grouped_grad = up * (gate * open_gate)
        gate_grad = up * (unit * gain + bias) * (open_gate * (1.0 + gate * (1.0 - open_gate)))
        grad_ref[rows, pl.ds(at_g, DV)] = gate_grad.astype(BF16)
        dgain = dgain + jnp.sum(grouped_grad * unit, axis=0, keepdims=True)
        dbias = dbias + jnp.sum(grouped_grad, axis=0, keepdims=True)
        unit_grad = grouped_grad * gain
        along = jnp.mean(unit_grad * unit, axis=-1, keepdims=True)
        level = jnp.mean(unit_grad, axis=-1, keepdims=True)
        retained_grad = (inverse * (unit_grad - level - unit * along)).astype(BF16)
        mask = mask_of(keyr_ref[rows, :], keyc_ref[...], decay, float(length)) * scale
        query = qr_ref[rows, :]
        weights = (dot_nt(query, kr_ref[...]) * mask).astype(BF16)
        value_part = dot_tn(weights, retained_grad)
        score_grad = (dot_nt(retained_grad, vb_ref[...]) * mask).astype(BF16)
        query_grad = dot_nn(score_grad, kr_ref[...])
        key_part = dot_tn(score_grad, query)
        if first == 0:
            dv_acc[...] = value_part
            dk_acc[...] = key_part
        else:
            dv_acc[...] += value_part
            dk_acc[...] += key_part
        grad_ref[rows, pl.ds(at_q, DK)] = turn(
            query_grad[:, :half], query_grad[:, half:], cos_ref[rows, :], -sin_ref[rows, :]
        )
    grad_ref[:, pl.ds(at_k, DK)] = turn(dk_acc[:, :half], dk_acc[:, half:], cos_ref[...], -sin_ref[...])
    grad_ref[:, pl.ds(at_v, DV)] = dv_acc[...].astype(BF16)
    dgain_ref[...] = dgain
    dbias_ref[...] = dbias


def retain_back(decays, keyr, keyc, cosine, sinusoid, qr, kr, vb, pre, kept, ups, gain, bias, place, heads):
    length = pre.shape[0]
    block = ups[0].shape[0]
    whole = lambda shape: pl.BlockSpec(shape, lambda h: (0,) * len(shape))
    cols = lambda width, start: pl.BlockSpec((length, width), lambda h: (0, start + h))
    vec = pl.BlockSpec((1, DV), lambda h: (0, h))
    return pl.pallas_call(
        retain_back_kernel,
        grid=(heads,),
        in_specs=[
            pl.BlockSpec(memory_space=pltpu.SMEM),
            whole((length, 1)), whole((1, length)),
            whole((length, DK // 2)), whole((length, DK // 2)),
            cols(DK, 0), cols(DK, 0), cols(DV, 0), cols(DV, 2 * heads), cols(DV, 0),
            vec, vec,
        ]
        + [pl.BlockSpec((block, DV), lambda h: (0, place * heads + h))] * len(ups),
        out_specs=[whole((length, heads * 2 * (DK + DV))), vec, vec],
        out_shape=[
            jax.ShapeDtypeStruct((length, heads * 2 * (DK + DV)), BF16),
            jax.ShapeDtypeStruct((1, heads * DV), F32),
            jax.ShapeDtypeStruct((1, heads * DV), F32),
        ],
        scratch_shapes=[pltpu.VMEM((length, DV), F32), pltpu.VMEM((length, DK), F32)],
        cost_estimate=pl.CostEstimate(
            flops=2 * heads * length * length * (3 * DK + 2 * DV),
            bytes_accessed=heads * length * (2 * DK * 4 + DV * 18),
            transcendentals=heads * length * length,
        ),
        name="retain_back",
    )(decays, keyr, keyc, cosine, sinusoid, qr, kr, vb, pre, kept, gain, bias, *ups)


def shards(
    span, batches,
    tokens, segment, ln1_gain, ln1_bias, w_query, w_key, w_value, w_gate, w_output, gn_gain, gn_bias,
    ln2_gain, ln2_bias, w_inner, b_inner, w_outer, b_outer, cotangent,
):
    fsdp, tp = span
    teams = tp // batches
    devices = fsdp * tp
    place = lax.axis_index("tp")
    mine = place // teams
    rank = place % teams
    width = tokens.shape[3]
    piece = tokens.shape[2]
    heads = w_query.shape[1] // DK
    units = w_inner.shape[1]
    channels = w_value.shape[1]

    def along_team(value, shift):
        route = [
            (i, (i // teams) * teams + (i % teams + shift) % teams) for i in range(tp)
        ]
        return lax.ppermute(value, "tp", route)

    def across(value, shift):
        route = [
            (i, ((i // teams + shift) % batches) * teams + i % teams) for i in range(tp)
        ]
        return lax.ppermute(value, "tp", route)

    def quarter(back_batch, back_rank):
        return ((mine + batches - back_batch) % batches) * teams + (rank + teams - back_rank) % teams

    def pick(array, shift):
        return lax.dynamic_index_in_dim(array, (mine + shift) % batches, 0, keepdims=False)

    def gather_team(value):
        return [value] + [along_team(value, s) for s in range(1, teams)]

    def send_parts(part_of):
        return [along_team(part_of(s).astype(BF16), teams - s) for s in range(1, teams)]

    def add_parts(total, sent, *fillers):
        held = lax.optimization_barrier((total, *sent, *fillers))
        total = held[0]
        for received in held[1 : 1 + len(sent)]:
            total = total + received.astype(F32)
        return total

    def give_back(rows):
        blocks = [rows[s * piece : (s + 1) * piece] for s in range(batches)]
        parts = [blocks[0]] + [
            across(blocks[s].astype(BF16), batches - s).astype(blocks[0].dtype) for s in range(1, batches)
        ]
        slots = []
        for i in range(batches):
            value = parts[0]
            for s in range(1, batches):
                value = jnp.where((mine + s) % batches == i, parts[s], value)
            slots.append(value)
        return jnp.stack(slots)[:, None]

    pieces = (ln1_gain, ln1_bias, ln2_gain, ln2_bias, b_outer, b_inner, gn_gain, gn_bias)
    flat = jnp.concatenate(pieces)
    used = flat.shape[0]
    lines = -(-used // 128)

    def exchange(table):
        padded = jnp.pad(table, ((0, 0), (0, lines * 128 - used))).reshape(devices, lines, 128)
        return lax.all_to_all(padded, ("fsdp", "tp"), 0, 0, tiled=True).reshape(devices, lines * 128)

    everyone = exchange(jnp.broadcast_to(flat[None], (devices, used)))
    vectors, begin = [], 0
    for item in pieces:
        vectors.append(everyone[:, begin : begin + item.shape[0]].reshape(-1))
        begin += item.shape[0]
    norm1_gain, norm1_bias, norm2_gain, norm2_bias, outer_bias, inner_all, group_gain_all, group_bias_all = vectors

    own_quarters = [quarter(s, 0) for s in range(batches)]

    def cut(vector, size):
        return [lax.dynamic_slice_in_dim(vector, q * size, size, 0) for q in own_quarters]

    inner_bias = jnp.concatenate(cut(inner_all, units))
    group_gains = [v[None] for v in cut(group_gain_all, channels)]
    group_biases = [v[None] for v in cut(group_bias_all, channels)]

    far = range(1, batches)
    mixer_shard = jnp.concatenate([w_query, w_key, w_value, w_gate], axis=1)
    token_pieces = [pick(tokens, 0)[0]] + [across(pick(tokens, s)[0], s) for s in far]
    mixer_shards = [mixer_shard] + [across(hold(mixer_shard, *token_pieces[1:]), s) for s in far]
    mixers = [lax.all_gather(s, "fsdp", axis=0, tiled=True) for s in mixer_shards]
    def both(shard, *after):
        return jnp.concatenate([shard] + [across(hold(shard, *after), s) for s in far], axis=1)

    def gather_rows(shard):
        return lax.all_gather(shard, "fsdp", axis=0, tiled=True)

    output_full = gather_rows(both(w_output.T, *mixer_shards[1:]))

    segments = pick(segment, 0)[0]
    length = segments.shape[0]
    position = doc_positions(segments)
    order = [quarter(s, r) for r in range(teams) for s in range(batches)]

    def ordered(vector):
        return jnp.concatenate([lax.dynamic_slice_in_dim(vector, q * piece, piece, 0) for q in order])

    index = jnp.arange(length, dtype=jnp.int32)
    keys = ordered((segments * (2 * length) + index).astype(F32))
    keyr, keyc = keys[:, None], keys[None, :]
    frequency = 10000.0 ** (-jnp.arange(DK // 2, dtype=F32) / (DK // 2))
    angles = ordered(position)[:, None] * frequency[None, :]
    cosine, sinusoid = jnp.cos(angles), jnp.sin(angles)
    decays = [
        jnp.log1p(-(2.0 ** (-5.0 - (q * heads + jnp.arange(heads, dtype=jnp.int32)).astype(F32))))
        for q in own_quarters
    ]

    normed_pieces = [
        layer_norm(t.astype(F32), norm1_gain, norm1_bias).astype(BF16) for t in token_pieces
    ]
    gathered = [gather_team(p) for p in normed_pieces]
    normed_one_all = jnp.concatenate(
        [gathered[s][r] for r in range(teams) for s in range(batches)], axis=0
    )
    rows_in = jnp.concatenate(token_pieces, axis=0).astype(F32)
    norm1_back = jax.vjp(layer_norm, rows_in, norm1_gain, norm1_bias)[1]
    inner_both, outer_both = both(w_inner, *mixer_shards[1:]), both(w_outer.T, *mixer_shards[1:])
    grad_pieces = [pick(cotangent, 0)[0]] + [
        across(hold(pick(cotangent, s)[0], inner_both, outer_both), s) for s in far
    ]
    grads_gathered = [gather_team(p) for p in grad_pieces]
    grad_blocks = [
        jnp.concatenate([grads_gathered[s][r] for s in range(batches)], axis=0) for r in range(teams)
    ]
    grad_rows = grad_blocks[0]
    gated = jnp.zeros((length, batches * channels), BF16)
    saved = []
    for s in range(batches):
        pre = dot_nn(normed_one_all, mixers[s])
        if s == 0:
            inner_full = gather_rows(hold(inner_both, pre))
        gated, kept, qr, kr, vb = retain(
            decays[s], keyr, keyc, cosine, sinusoid, pre, group_gains[s], group_biases[s], gated, s, heads
        )
        saved.append((pre, kept, qr, kr, vb))
    outer_full = gather_rows(hold(outer_both, pre))
    block = batches * piece

    def rows_of(array, r):
        return array[r * block : (r + 1) * block]

    def output_part(r):
        return dot_nt(rows_of(gated, r), output_full)

    sent = send_parts(output_part)
    hidden = rows_in + add_parts(output_part(0), sent)
    normed_two, norm2_back = jax.vjp(layer_norm, hidden, norm2_gain, norm2_bias)

    def activate(normed):
        inner = dot_nn(normed, inner_full) + inner_bias
        below = 0.5 * (1.0 + lax.erf(inner * (0.5**0.5)))
        bell = jnp.exp(-0.5 * inner * inner) * ((2.0 * jnp.pi) ** -0.5)
        return (inner * below).astype(BF16), (below + inner * bell).astype(BF16)

    normed_two_blocks = gather_team(normed_two.astype(BF16))
    first = activate(normed_two_blocks[0])
    normed_two_blocks[1:] = [hold(n, *first) for n in normed_two_blocks[1:]]
    active_blocks, slope_blocks = zip(first, *[activate(n) for n in normed_two_blocks[1:]])

    def inner_grad_of(r):
        return (slope_blocks[r].astype(F32) * dot_nn(grad_blocks[r], outer_full)).astype(BF16)

    inner_grad_blocks = [None] * teams
    sent = []
    for r in range(1, teams):
        inner_grad_blocks[r] = inner_grad_of(r)
        sent.append(along_team(dot_nt(inner_grad_blocks[r], inner_full).astype(BF16), teams - r))
    inner_grad_blocks[0] = inner_grad_of(0)

    def reduce_columns(whole):
        return lax.psum_scatter(whole, "fsdp", scatter_dimension=0, tiled=True)

    def trade(parts):
        return [parts[0]] + [across(parts[s], batches - s) for s in far]

    def settle(parts):
        total = parts[0].astype(F32)
        for part in parts[1:]:
            total = total + part.astype(F32)
        return total

    def settle_both(whole):
        size = whole.shape[1] // batches
        return settle(trade([whole[:, s * size : (s + 1) * size] for s in range(batches)]))

    active_all = jnp.concatenate(active_blocks, axis=0)
    grad_all = jnp.concatenate(grad_blocks, axis=0)
    outer_sum = dot_tn(grad_all, active_all).astype(BF16)
    normed_two_grad = add_parts(dot_nt(inner_grad_blocks[0], inner_full), sent, outer_sum)
    hidden_part, norm2_gain_sum, norm2_bias_sum = norm2_back(normed_two_grad)
    hidden_grad = grad_rows.astype(F32) + hidden_part
    hidden_low_blocks = gather_team(hidden_grad.astype(BF16))

    inner_grad_all = jnp.concatenate(inner_grad_blocks, axis=0)
    normed_two_all = jnp.concatenate(normed_two_blocks, axis=0)
    inner_sum = dot_tn(normed_two_all, inner_grad_all).astype(BF16)
    inner_bias_sum = jnp.sum(inner_grad_all.astype(F32), axis=0)
    outer_bias_sum = jnp.sum(grad_rows.astype(F32), axis=0)
    result_parts = [dot_nt(active_blocks[r], outer_full).astype(BF16) for r in range(1, teams)]
    result_own = dot_nt(active_blocks[0], outer_full)
    ups = [dot_nn(hidden_low_blocks[0], output_full)]
    hidden_low_blocks[1:] = [
        hold(h, inner_sum, ups[0], *result_parts) for h in hidden_low_blocks[1:]
    ]
    grad_outer = settle_both(reduce_columns(outer_sum)).T
    inner_reduced = reduce_columns(inner_sum)
    grad_inner = settle_both(inner_reduced)

    sent = [
        along_team(hold(p, *hidden_low_blocks[1:]), teams - 1 - i) for i, p in enumerate(result_parts)
    ]
    result = hidden + add_parts(result_own, sent) + outer_bias
    out = give_back(result.astype(BF16))

    ups += [dot_nn(h, output_full) for h in hidden_low_blocks[1:]]
    hidden_low_all = jnp.concatenate(hidden_low_blocks, axis=0)
    grads, gain_sums, bias_sums = [], [], []
    late, ready = (), ()
    for s in reversed(range(batches)):
        pre, kept, qr, kr, vb = saved[s]
        grad, gain_sum, bias_sum = retain_back(
            decays[s], keyr, keyc, cosine, sinusoid, hold(qr, *late, *ready), kr, vb, pre, kept, ups,
            group_gains[s], group_biases[s], s, heads,
        )
        grads.insert(0, grad)
        gain_sums.insert(0, gain_sum[0])
        bias_sums.insert(0, bias_sum[0])
        if s:
            late = late + (dot_tn(normed_one_all, grad).astype(BF16),)
            ready = (result, grad_outer)

    def normed_one_part(r):
        total = dot_nt(rows_of(grads[0], r), mixers[0])
        for s in far:
            total = total + dot_nt(rows_of(grads[s], r), mixers[s])
        return total

    sent = send_parts(normed_one_part)
    output_sum = dot_tn(hidden_low_all, gated).astype(BF16)
    far_sums = [reduce_columns(hold(m, inner_reduced)) for m in late[::-1]]
    own_sum = dot_tn(hold(normed_one_all, output_sum, grad_inner, *far_sums), grads[0]).astype(BF16)
    far_traded = trade([grads[0]] + far_sums)[1:]
    grad_output = settle_both(reduce_columns(output_sum)).T
    mixer_sums = [reduce_columns(own_sum)] + far_traded
    normed_one_grad = add_parts(normed_one_part(0), sent, output_sum, own_sum, *far_traded)
    input_part, norm1_gain_sum, norm1_bias_sum = norm1_back(normed_one_grad)
    input_grad = give_back(hidden_grad + input_part)
    grad_mixer = settle(mixer_sums)
    narrow, wide = w_query.shape[1], channels
    grad_query = grad_mixer[:, :narrow]
    grad_key = grad_mixer[:, narrow : 2 * narrow]
    grad_value = grad_mixer[:, 2 * narrow : 2 * narrow + wide]
    grad_gate = grad_mixer[:, 2 * narrow + wide :]

    def spread(parts, size):
        total = jnp.zeros((tp * size,), F32)
        for q, part in zip(own_quarters, parts):
            total = lax.dynamic_update_slice_in_dim(total, part, q * size, 0)
        return total

    sums = (
        norm1_gain_sum,
        norm1_bias_sum,
        norm2_gain_sum,
        norm2_bias_sum,
        outer_bias_sum,
        spread([inner_bias_sum[s * units : (s + 1) * units] for s in range(batches)], units),
        spread(gain_sums, channels),
        spread(bias_sums, channels),
    )
    shared = jnp.sum(exchange(jnp.concatenate([v.reshape(devices, -1) for v in sums], axis=1)), axis=0)
    small, begin = [], 0
    for item in pieces:
        small.append(shared[begin : begin + item.shape[0]])
        begin += item.shape[0]
    return (
        out, input_grad, small[0], small[1], grad_query, grad_key, grad_value, grad_gate, grad_output,
        small[6], small[7], small[2], small[3], grad_inner, small[5], grad_outer, small[4],
    )


def solution(mesh):
    rows, vec = P(None, "fsdp", "tp", None), P(("fsdp", "tp"))
    tall, flat = P("fsdp", "tp"), P("tp", "fsdp")
    span = (mesh.shape["fsdp"], mesh.shape["tp"])

    def step(*args):
        return jax.shard_map(
            functools.partial(shards, span, args[0].shape[0]),
            mesh=mesh,
            in_specs=(
                rows, P(None, "fsdp", None), vec, vec, tall, tall, tall, tall, flat,
                vec, vec, vec, vec, tall, vec, flat, vec, rows,
            ),
            out_specs=(
                rows, rows, vec, vec, tall, tall, tall, tall, flat,
                vec, vec, vec, vec, tall, vec, flat, vec,
            ),
            check_vma=False,
        )(*args)

    return step
```
